32 devices in a mesh: groups: 2 (over y), ctx: 8 (over z, core), heads: 2 (over x), rep: 1.
Axes of the slice: x: 2, y: 2, z: 4, core: 2. Of those that a mesh axis runs over, the one named last changes fastest.
Arguments:
- queries: bfloat16 [2048, 512], P(('groups', 'ctx'), ('heads', 'rep')), parts along dimension 0, may hold values from -2 to 2
- keys: bfloat16 [2048, 512], P(('groups', 'ctx'), ('heads', 'rep')), parts along dimension 0, may hold values from -2 to 2
- values: bfloat16 [2048, 512], P(('groups', 'ctx'), ('heads', 'rep')), parts along dimension 0, may hold values from -6 to 6
- doc_ids: int32 [2048], P(('groups', 'ctx')), parts along dimension 0, may hold values from 0 to 3, never falling along the last dimension, each value on 1 to 512 neighbouring positions
Outputs:
- attended: bfloat16 [2048, 512], P(('groups', 'ctx'), ('heads', 'rep')), parts along dimension 0
The draws below stay inside these ranges and needn't reach their ends.
There are 2 independent parts, one for each index of `groups`. The reference program is written for one: setup_inputs(seed, part) draws one part's arguments, and reference() takes and returns one part's arrays. A program takes and returns all parts, laid end to end along the dimension named above; each array names one. Nothing has to cross between parts.
Inputs may be any that keep to these rules, and one draw needn't show every extreme that they name: `doc_ids`: document numbers never fall along the sequence and every number appears; each document has 1 to 512 tokens, and one has exactly 512.
All inputs are finite; a program needn't handle non-finite values.
Results may differ from the reference program's by a relative error of at most 0.0054.
Values sent between devices are 32-bit elements; how exact they have to be, the bound alone decides.
No kernel may reach another device: no remote copies, remote signals or barrier semaphores. Data moves between devices by JAX's collectives and lax.ppermute only.
A program may use at most 64 MiB of HBM per device.

```python
import math
import jax
import jax.numpy as jnp
import numpy as np
from jax import lax

HW = 64
TOK_DEV = 128
HEADS = 8
FEAT = 2080
NSEQ = 1024
MOST = 512
DOCS = 4


def block_scale(stream_key, extent, shards, least, largest):
    def one(position, shards_of):
        draws = jax.random.uniform(jax.random.fold_in(jax.random.fold_in(stream_key, 6), position), (shards_of,), jnp.float32, least / len(shards), largest / len(shards))
        return jnp.repeat(jnp.exp(draws), extent[position] // shards_of).reshape((-1,) + (1,) * (len(extent) - position - 1))

    level = one(*shards[0])
    for cut in shards[1:]:
        level = level * one(*cut)
    return level


def split_up(amount, total, bound, slope):
    portions = [(1 << 20) // math.isqrt(standing ** slope) + 1 for standing in range(2, amount + 1)]
    surplus, counts = total - bound - (amount - 1), [1] * (amount - 1)
    while surplus > 0:
        candidates = [i for i in range(amount - 1) if counts[i] < bound]
        whole, budget = sum([portions[i] for i in candidates]), surplus
        for i in candidates:
            addition = min(bound - counts[i], max(1, budget * portions[i] // whole), surplus)
            counts[i] = counts[i] + addition
            surplus = surplus - addition
    return np.array([bound] + counts)


def ragged_sizes(rng, count, total, bound, slope):
    if count == 2:
        one = jax.random.randint(rng, (), max(1, total - bound), min(bound, total - 1) + 1)
        return jnp.stack([one, total - one])
    lengths = jnp.asarray(split_up(count, total, bound, slope), jnp.int32)
    pairs = (count - 1) // 2
    donor, taker = lengths[1:1 + 2 * pairs:2], lengths[2:2 + 2 * pairs:2]
    room = jnp.minimum(donor - 1, bound - taker)
    moved = jax.random.randint(jax.random.fold_in(rng, 1), (pairs,), 0, 1 << 20) % (room + 1)
    lengths = lengths.at[1:1 + 2 * pairs:2].set(donor - moved).at[2:2 + 2 * pairs:2].set(taker + moved)
    return lengths[jax.random.permutation(jax.random.fold_in(rng, 2), count)]


def gaussian(own_key, extent, deviation, bound, cuts=(), kind=jnp.bfloat16):
    factor_of = block_scale(own_key, extent, cuts, -0.22, 0.18) if cuts else 1.0
    values = jax.random.normal(own_key, extent, jnp.float32) * deviation * factor_of
    return jnp.minimum(jnp.maximum(values, -bound), bound).astype(kind)


def setup_inputs(seed: int = 0, part: int = 0) -> dict:
    splits = jax.random.split(jax.random.key(seed), 5)
    part_keys = jax.random.split(jax.random.fold_in(splits[4], part), 5)
    queries = gaussian(part_keys[0], (NSEQ, HEADS * HW), 0.35, 2.0, ((0, 8), (1, 2)))
    keys = gaussian(part_keys[1], (NSEQ, HEADS * HW), 0.35, 2.0, ((0, 8), (1, 2)))
    values = gaussian(part_keys[2], (NSEQ, HEADS * HW), 1.0, 6.0, ((0, 8), (1, 2)))
    doc_ids = jnp.searchsorted(jnp.cumsum(ragged_sizes(part_keys[3], DOCS, NSEQ, MOST, 2)), jnp.arange(NSEQ), side="right").astype(jnp.int32)
    return {"queries": queries, "keys": keys, "values": values, "doc_ids": doc_ids}


def expand(rows_in):
    breadth = rows_in.shape[-1]
    pieces = []
    for column in range(breadth):
        factor = jnp.where(jnp.arange(breadth - column) == 0, 1.0, math.sqrt(2.0)).astype(rows_in.dtype)
        pieces.append(rows_in[..., column:column + 1] * rows_in[..., column:] * factor)
    return jnp.concatenate(pieces, axis=-1)

def reference(queries, keys, values, doc_ids):
    seq_total = queries.shape[0]
    nblocks = seq_total // TOK_DEV

    def to_blocks(array_in):
        return array_in.reshape(nblocks, TOK_DEV, HEADS, HW).transpose(0, 2, 1, 3)
    q_all = to_blocks(queries)
    k_all = to_blocks(keys)
    v_all = to_blocks(values)
    id_all = doc_ids.reshape(nblocks, TOK_DEV)
    row_pos = jnp.arange(TOK_DEV)
    causal = row_pos[:, None] >= row_pos[None, :]

    def one_block(run_carry, inputs):
        run_state, run_sid = run_carry
        q_blk, k_blk, v_blk, block_ids = inputs
        first_id = block_ids[0]
        last_id = block_ids[TOK_DEV - 1]
        carried = jnp.where(run_sid == first_id, run_state, jnp.zeros_like(run_state)).astype(jnp.bfloat16)
        in_last = (block_ids == last_id)[:, None]
        first_rows = (block_ids == first_id)[:, None]
        allowed = causal & (block_ids[:, None] == block_ids[None, :])

        def head_work(head_items):
            q_one, k_one, v_one, carry_one = head_items
            phi_k = expand(k_one.astype(jnp.float32)).astype(jnp.bfloat16)
            masked = jnp.where(in_last, v_one, jnp.zeros_like(v_one))
            head_state = jnp.dot(phi_k.T, masked, preferred_element_type=jnp.float32)
            scores = jnp.dot(q_one, k_one.T, preferred_element_type=jnp.float32)
            weights = jnp.where(allowed, scores * scores, jnp.zeros_like(scores)).astype(jnp.bfloat16)
            intra_part = jnp.dot(weights, v_one, preferred_element_type=jnp.float32)
            phi_q = expand(q_one.astype(jnp.float32)).astype(jnp.bfloat16)
            readout = jnp.dot(phi_q, carry_one, preferred_element_type=jnp.float32)
            summed = intra_part + jnp.where(first_rows, readout, jnp.zeros_like(readout))
            normed = summed * lax.rsqrt(lax.optimization_barrier(jnp.mean(summed * summed, axis=-1, keepdims=True)) + 1e-06)
            return (normed.astype(jnp.bfloat16), head_state)
        block_outs, states = lax.map(head_work, (q_blk, k_blk, v_blk, carried))
        new_state = states + jnp.where(run_sid == last_id, run_state, jnp.zeros_like(run_state))
        return ((new_state, last_id), block_outs)
    start_carry = (jnp.zeros((HEADS, FEAT, HW), jnp.float32), jnp.array(-1, jnp.int32))
    final_carry, block_outs = lax.scan(one_block, start_carry, (q_all, k_all, v_all, id_all))
    return block_outs.transpose(0, 2, 1, 3).reshape(seq_total, HEADS * HW)
```

```python
import functools

import jax
import jax.numpy as jnp
from jax import lax
from jax.experimental import pallas as pl
from jax.experimental.pallas import tpu as pltpu
from jax.sharding import PartitionSpec as P

HW = 64
MOST = 512
LANES = 128
TILE = 8
EPS = 1e-06
GRANT = 16 << 20


def chip_moves(length, first):
    couples = length // 2
    cycle = couples - first
    pairs = []
    for couple in range(couples):
        for side in range(2):
            if couple < first or cycle < 2:
                pairs.append((2 * couple + side, 2 * couple + 1 - side))
            else:
                target = couple + 1 if couple + 1 < couples else first
                pairs.append((2 * couple + side, 2 * target + side))
    return pairs


def trade(x):
    length = lax.axis_size("ctx")
    return lax.ppermute(x, "ctx", [(i, i ^ 1) for i in range(length)])


def lower_half(shape):
    return lax.broadcasted_iota(jnp.int32, shape, 1) % LANES < HW


def two_heads(block):
    low = lower_half(block.shape)
    zero = jnp.zeros_like(block)
    both = jnp.concatenate([jnp.where(low, block, zero), jnp.where(low, zero, block)], axis=0)
    return both.astype(jnp.bfloat16)


def attend(q_two, k_block, v_block, mask):
    scores = lax.dot_general(
        q_two, two_heads(k_block), (((1,), (1,)), ((), ())), preferred_element_type=jnp.float32
    )
    weights = jnp.where(mask, scores * scores, jnp.zeros_like(scores)).astype(jnp.bfloat16)
    return jnp.dot(weights, two_heads(v_block), preferred_element_type=jnp.float32)


def head_pair(ref, pair, rows):
    return ref[pair * rows : (pair + 1) * rows, :]


def pack_body(k_ref, v_ref, ids_ref, kp_ref, vp_ref):
    rows = k_ref.shape[0]
    for pair in range(k_ref.shape[1] // LANES):
        cut = slice(pair * LANES, (pair + 1) * LANES)
        kp_ref[pair * rows : (pair + 1) * rows, :] = k_ref[:, cut].astype(jnp.float32)
        vp_ref[pair * rows : (pair + 1) * rows, :] = v_ref[:, cut].astype(jnp.float32)
    ids = ids_ref[...].astype(jnp.float32)
    kp_ref[kp_ref.shape[0] - TILE :, :] = jnp.broadcast_to(ids, (TILE, rows))


def earlier_blocks(q_ref, ids_ref, blocks):
    rows = q_ref.shape[0]
    ids = ids_ref[...].astype(jnp.float32)
    first = ids[:, 0:1]
    count = jnp.sum(jnp.where(ids == first, 1.0, 0.0), axis=1, keepdims=True)
    seen = lax.broadcasted_iota(jnp.int32, (rows, LANES), 0).astype(jnp.float32) < count
    parts = []
    for pair in range(q_ref.shape[1] // LANES):
        q_two = q_ref[:, pair * LANES : (pair + 1) * LANES]
        total = jnp.zeros((rows, LANES), jnp.float32)
        for k_ref, v_ref, usable in blocks:
            top = k_ref.shape[0] - TILE
            there = k_ref[top : top + 1, :]
            mask = jnp.where(usable, there, -1.0) == first
            mask = jnp.concatenate([mask, mask], axis=1)
            total = total + attend(
                q_two, head_pair(k_ref, pair, rows), head_pair(v_ref, pair, rows), mask
            )
        parts.append(jnp.where(seen, total, jnp.zeros_like(total)))
    return parts


def local_body(q_ref, k_ref, v_ref, ids_ref, sk_ref, sv_ref, y_ref):
    rows = q_ref.shape[0]
    odd = lax.axis_index("ctx") % 2 == 1
    ids = ids_ref[...].astype(jnp.float32)
    row_pos = lax.broadcasted_iota(jnp.int32, (rows, rows), 0)
    col_pos = lax.broadcasted_iota(jnp.int32, (rows, rows), 1)
    tall = jnp.sum(jnp.where(row_pos == col_pos, ids, 0.0), axis=1, keepdims=True)
    allowed = (row_pos >= col_pos) & (tall == ids)
    allowed = jnp.concatenate([allowed, allowed], axis=1)
    far = earlier_blocks(q_ref, ids_ref, [(sk_ref, sv_ref, odd)])
    for pair in range(q_ref.shape[1] // LANES):
        cut = slice(pair * LANES, (pair + 1) * LANES)
        near = attend(
            q_ref[:, cut],
            k_ref[:, cut].astype(jnp.float32),
            v_ref[:, cut].astype(jnp.float32),
            allowed,
        )
        y_ref[pair * rows : (pair + 1) * rows, :] = near + far[pair]


def add_body(back, q_ref, ids_ref, y_ref, k_ref, v_ref, sk_ref, sv_ref, o_ref):
    rows = q_ref.shape[0]
    usable = lax.axis_index("ctx") >= 2 * back
    far = earlier_blocks(q_ref, ids_ref, [(k_ref, v_ref, usable), (sk_ref, sv_ref, usable)])
    for pair in range(q_ref.shape[1] // LANES):
        o_ref[pair * rows : (pair + 1) * rows, :] = head_pair(y_ref, pair, rows) + far[pair]


def last_body(back, q_ref, ids_ref, y_ref, k_ref, v_ref, sk_ref, sv_ref, o_ref):
    rows = q_ref.shape[0]
    usable = lax.axis_index("ctx") >= 2 * back
    far = earlier_blocks(q_ref, ids_ref, [(k_ref, v_ref, usable), (sk_ref, sv_ref, usable)])
    low = lower_half((rows, LANES))
    for pair in range(q_ref.shape[1] // LANES):
        y = head_pair(y_ref, pair, rows) + far[pair]
        square = y * y
        sum_low = jnp.sum(jnp.where(low, square, 0.0), axis=1, keepdims=True)
        sum_high = jnp.sum(jnp.where(low, 0.0, square), axis=1, keepdims=True)
        mean = jnp.where(low, sum_low, sum_high) * (1.0 / HW)
        o_ref[:, pair * LANES : (pair + 1) * LANES] = (y * lax.rsqrt(mean + EPS)).astype(o_ref.dtype)


def call(body, out, name, flops, *args):
    moved = sum(a.size * a.dtype.itemsize for a in args)
    return pl.pallas_call(
        body,
        out_shape=out,
        name=name,
        cost_estimate=pl.CostEstimate(flops=flops, bytes_accessed=moved, transcendentals=0),
        compiler_params=pltpu.CompilerParams(vmem_limit_bytes=GRANT),
    )(*args)


def per_device(queries, keys, values, doc_ids):
    rows, columns = queries.shape
    assert columns % LANES == 0 and rows == LANES
    length = lax.axis_size("ctx")
    assert length % 2 == 0
    reach = -(-MOST // rows)
    hops = -(-reach // 2)
    pairs = columns // LANES
    flat = pairs * rows
    one = 4 * rows * rows * columns
    ids = doc_ids.reshape(1, rows)
    y_shape = jax.ShapeDtypeStruct((flat, LANES), jnp.float32)
    packed = (jax.ShapeDtypeStruct((flat + TILE, LANES), jnp.float32), y_shape)
    k_now, v_now = call(pack_body, packed, "pack", 0, keys, values, ids)
    k_side, v_side = trade(k_now), trade(v_now)
    y = call(local_body, y_shape, "local", 2 * one, queries, keys, values, ids, k_side, v_side)
    for back in range(1, hops + 1):
        moves = chip_moves(length, back - 1)
        k_now, v_now = lax.ppermute(k_now, "ctx", moves), lax.ppermute(v_now, "ctx", moves)
        k_side, v_side = trade(k_now), trade(v_now)
        last = back == hops
        body = functools.partial(last_body if last else add_body, back)
        out = jax.ShapeDtypeStruct((rows, columns), jnp.bfloat16) if last else y_shape
        y = call(body, out, f"far{back}", 2 * one, queries, ids, y, k_now, v_now, k_side, v_side)
    return y


def solution(mesh):
    placed = P(("groups", "ctx"), ("heads", "rep"))
    return jax.shard_map(
        per_device,
        mesh=mesh,
        in_specs=(placed, placed, placed, P(("groups", "ctx"))),
        out_specs=placed,
        check_vma=False,
    )
```

```python
import functools

import jax
import jax.numpy as jnp
from jax import lax
from jax.experimental import pallas as pl
from jax.experimental.pallas import tpu as pltpu
from jax.sharding import PartitionSpec as P


HW = 64
MOST = 512
LANES = 128
TILE = 8
EPS = 1e-06
GRANT = 16 << 20


def snake(x, rising, first):
    couples = lax.axis_size("ctx") // 2
    pairs = []
    for couple in range(couples):
        up, down = 2 * couple + rising, 2 * couple + 1 - rising
        pairs.append((up, up + 2 if first <= couple < couples - 1 else down))
        pairs.append((down, down - 2 if couple > first else up))
    return lax.ppermute(x, "ctx", pairs)


def climb(x, first):
    couples = lax.axis_size("ctx") // 2
    pairs = []
    for couple in range(couples):
        for side in range(2):
            here, stay = 2 * couple + side, couple < first or couples - first < 2
            target = couple + 1 if couple + 1 < couples else first
            pairs.append((here, here ^ 1 if stay else 2 * target + side))
    return lax.ppermute(x, "ctx", pairs)


def rise(x, first):
    length = lax.axis_size("ctx")
    return lax.ppermute(x, "ctx", [(i, i + 2) for i in range(2 * first, length - 2)])


def trade(x):
    return lax.ppermute(x, "ctx", [(i, i ^ 1) for i in range(lax.axis_size("ctx"))])


def is_odd():
    return lax.axis_index("ctx") % 2 == 1


def lower_half(shape):
    return lax.broadcasted_iota(jnp.int32, shape, 1) % LANES < HW


def two_heads(block):
    low = lower_half(block.shape)
    zero = jnp.zeros_like(block)
    both = jnp.concatenate([jnp.where(low, block, zero), jnp.where(low, zero, block)], axis=0)
    return both.astype(jnp.bfloat16)


def attend(q_two, keys, values, mask):
    scores = lax.dot_general(
        q_two, two_heads(keys), (((1,), (1,)), ((), ())), preferred_element_type=jnp.float32
    )
    mask = jnp.concatenate([mask, mask], axis=1)
    weights = jnp.where(mask, scores * scores, jnp.zeros_like(scores)).astype(jnp.bfloat16)
    return jnp.dot(weights, two_heads(values), preferred_element_type=jnp.float32)


def pick(flag, this, other, start, size):
    return jnp.where(flag, this[start : start + size, :], other[start : start + size, :])


def pick_ids(flag, this, other):
    return pick(flag, this, other, this.shape[0] - TILE, 1)


def pick_pair(flag, these, others, pair, rows):
    this, other = these[pair], others[pair]
    return pick(flag, this, other, 0, rows), pick(flag, this, other, rows, rows)


def rows_of_first(ids):
    count = jnp.sum(jnp.where(ids == ids[:, 0:1], 1.0, 0.0), axis=1, keepdims=True)
    shape = (ids.shape[1], LANES)
    return lax.broadcasted_iota(jnp.int32, shape, 0).astype(jnp.float32) < count


def cut(pair):
    return slice(pair * LANES, (pair + 1) * LANES)


def groups_of(refs, count, pairs):
    return [refs[at * pairs : (at + 1) * pairs] for at in range(count)], refs[count * pairs :]


def pack_body(pairs, k_hbm, v_hbm, q_hbm, ids_hbm, high, low, *refs):
    rest, (own_ref, k_ref, v_ref, q_ref, ids_ref, sem) = refs[: pairs - 1], refs[pairs - 1 :]
    rows = k_ref.shape[0]
    moves = []
    routes = [(k_hbm, k_ref), (v_hbm, v_ref), (q_hbm, q_ref), (ids_hbm, ids_ref)]
    for at, (source, target) in enumerate(routes):
        moves.append(pltpu.make_async_copy(source, target, sem.at[at]))
        moves[-1].start()
    for item in moves:
        item.wait()
    ids = ids_ref[...].astype(jnp.float32)
    own_ref[...] = ids
    wide = jnp.broadcast_to(ids, (TILE, rows))
    odd = is_odd()

    def put(target, pair):
        target[:rows, :] = k_ref[:, cut(pair)].astype(jnp.float32)
        target[rows : 2 * rows, :] = v_ref[:, cut(pair)].astype(jnp.float32)

    def fill(up, down):
        size = up.shape[0] - TILE
        put(up, 0)
        for pair in range(pairs):
            down[pair * rows : (pair + 1) * rows, :] = q_ref[:, cut(pair)].astype(jnp.float32)
        for target, done in ((up, 2 * rows), (down, pairs * rows)):
            if done < size:
                target[done:size, :] = jnp.zeros((size - done, LANES), jnp.float32)
            target[size:, :] = wide

    @pl.when(odd)
    def _():
        fill(high, low)

    @pl.when(jnp.logical_not(odd))
    def _():
        fill(low, high)

    for pair in range(1, pairs):
        put(rest[pair - 1], pair)


def local_body(pairs, q_ref, *refs):
    (high, low, side), (y_ref,) = groups_of(refs, 3, pairs)
    rows = q_ref.shape[0]
    odd = is_odd()
    ids = pick_ids(odd, high[0], low[0])
    row_pos = lax.broadcasted_iota(jnp.int32, (rows, rows), 0)
    col_pos = lax.broadcasted_iota(jnp.int32, (rows, rows), 1)
    tall = jnp.sum(jnp.where(row_pos == col_pos, ids, 0.0), axis=1, keepdims=True)
    allowed = (row_pos >= col_pos) & (tall == ids)
    seen = rows_of_first(ids)
    before = jnp.where(odd, pick_ids(odd, side[0], side[0]), -1.0) == ids[:, 0:1]
    for pair in range(pairs):
        q_two = q_ref[:, cut(pair)]
        near = attend(q_two, *pick_pair(odd, high, low, pair, rows), allowed)
        earlier = attend(q_two, *pick_pair(odd, side, side, pair, rows), before)
        y_ref[pair * rows : (pair + 1) * rows, :] = near + jnp.where(seen, earlier, 0.0)


def finish(y, o_ref, pair):
    low = lower_half(y.shape)
    square = y * y
    sum_low = jnp.sum(jnp.where(low, square, 0.0), axis=1, keepdims=True)
    sum_high = jnp.sum(jnp.where(low, 0.0, square), axis=1, keepdims=True)
    mean = jnp.where(low, sum_low, sum_high) * (1.0 / HW)
    o_ref[:, cut(pair)] = (y * lax.rsqrt(mean + EPS)).astype(o_ref.dtype)


def deliver(o_ref, o_hbm, sem):
    copy = pltpu.make_async_copy(o_ref, o_hbm, sem)
    copy.start()
    copy.wait()


def has_far():
    return lax.axis_index("ctx") >= 4


def near_body(pairs, q_ref, own_ref, y_ref, *refs):
    (high, low, high_side, low_side), (t_ref, o_hbm, o_ref, sem) = groups_of(refs, 4, pairs)
    rows = q_ref.shape[0]
    odd = is_odd()
    usable = lax.axis_index("ctx") >= 2
    ids = own_ref[...]
    seen = rows_of_first(ids)
    sources = ((high, low), (low_side, high_side))
    masks = [
        jnp.where(usable, pick_ids(odd, this[0], other[0]), -1.0) == ids[:, 0:1]
        for this, other in sources
    ]
    for pair in range(pairs):
        q_two = q_ref[:, cut(pair)]
        total = jnp.zeros((rows, LANES), jnp.float32)
        for (this, other), mask in zip(sources, masks, strict=True):
            total = total + attend(q_two, *pick_pair(odd, this, other, pair, rows), mask)
        span = slice(pair * rows, (pair + 1) * rows)
        t_ref[span, :] = y_ref[span, :] + jnp.where(seen, total, 0.0)

    @pl.when(jnp.logical_not(has_far()))
    def _():
        for pair in range(pairs):
            finish(t_ref[pair * rows : (pair + 1) * rows, :], o_ref, pair)
        deliver(o_ref, o_hbm, sem)


def far_body(pair, high0, low0, side0, high, low, side, o_ref):
    rows = o_ref.shape[0]
    odd = is_odd()
    first = pick_ids(odd, low0, high0)[:, 0:1]
    near_mask = pick_ids(odd, high0, low0) == first
    side_mask = jnp.where(odd, -1.0, pick_ids(odd, side0, side0)) == first
    q_two = pick(odd, low0, high0, pair * rows, rows).astype(jnp.bfloat16)
    total = attend(q_two, *pick_pair(odd, [high], [low], 0, rows), near_mask)
    o_ref[...] = total + attend(q_two, *pick_pair(odd, [side], [side], 0, rows), side_mask)


def far_all(pairs, *refs):
    (high, low, side), (o_ref,) = groups_of(refs, 3, pairs)
    rows = o_ref.shape[0] // pairs
    for pair in range(pairs):
        far_body(
            pair, high[0], low[0], side[0], high[pair], low[pair], side[pair],
            o_ref.at[pair * rows : (pair + 1) * rows, :],
        )


def last_body(pairs, own_ref, y_ref, _, *refs):
    far, (o_hbm, o_ref, sem) = refs[: 2 * pairs], refs[2 * pairs :]
    rows = o_ref.shape[0]

    @pl.when(has_far())
    def _():
        odd = is_odd()
        seen = rows_of_first(own_ref[...])
        for pair in range(pairs):
            start = pair * rows if far[0].shape[0] > rows else 0
            came = pick(odd, far[2 * pair], far[2 * pair + 1], start, rows)
            y = y_ref[pair * rows : (pair + 1) * rows, :] + jnp.where(seen, came, 0.0)
            finish(y, o_ref, pair)
        deliver(o_ref, o_hbm, sem)


def call(body, out, flops, *args, **extra):
    moved = sum(a.size * a.dtype.itemsize for a in args)
    return pl.pallas_call(
        body,
        out_shape=out,
        cost_estimate=pl.CostEstimate(flops=flops, bytes_accessed=moved, transcendentals=0),
        compiler_params=pltpu.CompilerParams(vmem_limit_bytes=GRANT),
        **extra,
    )(*args)


def f32(*shape):
    return jax.ShapeDtypeStruct(shape, jnp.float32)


def per_device(queries, keys, values, doc_ids):
    rows, columns = queries.shape
    assert columns % LANES == 0 and rows == LANES and lax.axis_size("ctx") % 2 == 0
    assert MOST <= 4 * rows
    pairs = columns // LANES
    one = 4 * rows * rows * LANES
    ids = doc_ids.reshape(1, rows)
    held = [pltpu.with_memory_space_constraint(x, pltpu.HBM) for x in (keys, values, queries, ids)]
    load = f32(max(2, pairs) * rows + TILE, LANES)
    y_shape = f32(pairs * rows, LANES)
    every = range(pairs)

    def work(body, out, flops, *args):
        return call(functools.partial(body, pairs), out, flops, *args)

    def each(moved, arrays):
        out = []
        for pair in every:
            out.append(None if arrays[pair] is None else moved(arrays[pair]))
        return out

    high, low, *rest, own = call(
        functools.partial(pack_body, pairs),
        (load, load, *[f32(2 * rows, LANES)] * (pairs - 1), f32(1, rows)),
        0,
        *held,
        in_specs=[pl.BlockSpec(memory_space=pltpu.HBM)] * 4,
        scratch_shapes=[pltpu.VMEM((rows, columns), x.dtype) for x in (keys, values, queries)]
        + [pltpu.VMEM((1, rows), ids.dtype), pltpu.SemaphoreType.DMA((4,))],
    )
    highs, lows = [high, *rest], [low, *rest]
    got_high = [snake(high, 1, 0)]
    got_low = [snake(low, 0, 0)]
    for pair in range(1, pairs):
        if UP == "S":
            got_high.append(snake(rest[pair - 1], 1, 0))
            got_low.append(snake(rest[pair - 1], 0, 0))
        else:
            got_high.append((climb if UP == "C" else rise)(rest[pair - 1], 0))
            got_low.append(got_high[-1])
    side = each(trade, lows)
    high_side = each(trade, got_high)
    low_side = []
    for pair in every:
        if pair and UP != "S":
            low_side.append(high_side[pair])
        else:
            low_side.append(trade(got_low[pair]))
    lead = (got_high[0], got_low[0], high_side[0])

    def backs(value, kind):
        if kind == "T":
            one_way = snake(value, 1, 1)
            return [one_way, snake(value, 0, 1)]
        return [(climb if kind == "C" else rise)(value, 1)] * 2

    back = []
    if len(BACK) == 1:
        far = call(
            functools.partial(far_all, pairs), y_shape, 4 * pairs * one,
            *got_high, *got_low, *high_side,
        )
        back = backs(far, BACK) * pairs
    else:
        for pair in every:
            args = (*lead, got_high[pair], got_low[pair], high_side[pair])
            body = functools.partial(far_body, pair)
            far = call(body, f32(rows, LANES), 4 * one, *args)
            back += backs(far, BACK[pair])
    y = work(local_body, y_shape, 4 * pairs * one, queries, *highs, *lows, *side)
    out = jax.ShapeDtypeStruct((rows, columns), queries.dtype)
    staged = [pltpu.VMEM(out.shape, out.dtype), pltpu.SemaphoreType.DMA(())]
    here, there = pl.BlockSpec(memory_space=pltpu.VMEM), pl.BlockSpec(memory_space=pltpu.HBM)
    y, out_so_far = call(
        functools.partial(near_body, pairs),
        (y_shape, out),
        4 * pairs * one,
        queries,
        own,
        y,
        *got_high,
        *got_low,
        *high_side,
        *low_side,
        out_specs=(here, there),
        scratch_shapes=staged,
    )
    return call(
        functools.partial(last_body, pairs),
        out,
        0,
        own,
        y,
        out_so_far,
        *back,
        in_specs=[here, here, there] + [here] * len(back),
        out_specs=there,
        scratch_shapes=staged,
        input_output_aliases={2: 0},
    )


UP = "C"
BACK = 'CC'


def solution(mesh):
    placed = P(("groups", "ctx"), ("heads", "rep"))
    return jax.shard_map(
        per_device,
        mesh=mesh,
        in_specs=(placed, placed, placed, P(("groups", "ctx"))),
        out_specs=placed,
        check_vma=False,
    )
```

```python
import functools

import jax
import jax.numpy as jnp
from jax import lax
from jax.experimental import pallas as pl
from jax.experimental.pallas import tpu as pltpu
from jax.sharding import PartitionSpec as P


HW = 64
MOST = 512
LANES = 128
TILE = 8
EPS = 1e-06
GRANT = 16 << 20


def snake(x, rising, first):
    couples = lax.axis_size("ctx") // 2
    pairs = []
    for couple in range(couples):
        up, down = 2 * couple + rising, 2 * couple + 1 - rising
        pairs.append((up, up + 2 if first <= couple < couples - 1 else down))
        pairs.append((down, down - 2 if couple > first else up))
    return lax.ppermute(x, "ctx", pairs)


def climb(x, first):
    couples = lax.axis_size("ctx") // 2
    pairs = []
    for couple in range(couples):
        for side in range(2):
            here, stay = 2 * couple + side, couple < first or couples - first < 2
            target = couple + 1 if couple + 1 < couples else first
            pairs.append((here, here ^ 1 if stay else 2 * target + side))
    return lax.ppermute(x, "ctx", pairs)


def rise(x, first):
    length = lax.axis_size("ctx")
    return lax.ppermute(x, "ctx", [(i, i + 2) for i in range(2 * first, length - 2)])


def trade(x):
    return lax.ppermute(x, "ctx", [(i, i ^ 1) for i in range(lax.axis_size("ctx"))])


def is_odd():
    return lax.axis_index("ctx") % 2 == 1


def lower_half(shape):
    return lax.broadcasted_iota(jnp.int32, shape, 1) % LANES < HW


def two_heads(block):
    low = lower_half(block.shape)
    zero = jnp.zeros_like(block)
    both = jnp.concatenate([jnp.where(low, block, zero), jnp.where(low, zero, block)], axis=0)
    return both.astype(jnp.bfloat16)


def attend(q_two, keys, values, mask):
    scores = lax.dot_general(
        q_two, two_heads(keys), (((1,), (1,)), ((), ())), preferred_element_type=jnp.float32
    )
    mask = jnp.concatenate([mask, mask], axis=1)
    weights = jnp.where(mask, scores * scores, jnp.zeros_like(scores)).astype(jnp.bfloat16)
    return jnp.dot(weights, two_heads(values), preferred_element_type=jnp.float32)


def pick(flag, this, other, start, size):
    return jnp.where(flag, this[start : start + size, :], other[start : start + size, :])


def pick_ids(flag, this, other):
    return pick(flag, this, other, this.shape[0] - TILE, 1)


def pick_pair(flag, these, others, pair, rows):
    this, other = these[pair], others[pair]
    return pick(flag, this, other, 0, rows), pick(flag, this, other, rows, rows)


def rows_of_first(ids):
    count = jnp.sum(jnp.where(ids == ids[:, 0:1], 1.0, 0.0), axis=1, keepdims=True)
    shape = (ids.shape[1], LANES)
    return lax.broadcasted_iota(jnp.int32, shape, 0).astype(jnp.float32) < count


def cut(pair):
    return slice(pair * LANES, (pair + 1) * LANES)


def groups_of(refs, count, pairs):
    return [refs[at * pairs : (at + 1) * pairs] for at in range(count)], refs[count * pairs :]


def pack_body(pairs, k_hbm, v_hbm, q_hbm, ids_hbm, high, low, *refs):
    rest, (own_ref, k_ref, v_ref, q_ref, ids_ref, sem) = refs[: pairs - 1], refs[pairs - 1 :]
    rows = k_ref.shape[0]
    moves = []
    routes = [(k_hbm, k_ref), (v_hbm, v_ref), (q_hbm, q_ref), (ids_hbm, ids_ref)]
    for at, (source, target) in enumerate(routes):
        moves.append(pltpu.make_async_copy(source, target, sem.at[at]))
        moves[-1].start()
    for item in moves:
        item.wait()
    ids = ids_ref[...].astype(jnp.float32)
    own_ref[...] = ids
    wide = jnp.broadcast_to(ids, (TILE, rows))
    odd = is_odd()

    def put(target, pair):
        target[:rows, :] = k_ref[:, cut(pair)].astype(jnp.float32)
        target[rows : 2 * rows, :] = v_ref[:, cut(pair)].astype(jnp.float32)

    def fill(up, down):
        size = up.shape[0] - TILE
        put(up, 0)
        for pair in range(pairs):
            down[pair * rows : (pair + 1) * rows, :] = q_ref[:, cut(pair)].astype(jnp.float32)
        for target, done in ((up, 2 * rows), (down, pairs * rows)):
            if done < size:
                target[done:size, :] = jnp.zeros((size - done, LANES), jnp.float32)
            target[size:, :] = wide

    @pl.when(odd)
    def _():
        fill(high, low)

    @pl.when(jnp.logical_not(odd))
    def _():
        fill(low, high)

    for pair in range(1, pairs):
        put(rest[pair - 1], pair)


def local_body(pairs, q_ref, *refs):
    (high, low, side), (y_ref, o_hbm, o_ref, sem) = groups_of(refs, 3, pairs)
    rows = q_ref.shape[0]
    odd = is_odd()
    ids = pick_ids(odd, high[0], low[0])
    row_pos = lax.broadcasted_iota(jnp.int32, (rows, rows), 0)
    col_pos = lax.broadcasted_iota(jnp.int32, (rows, rows), 1)
    tall = jnp.sum(jnp.where(row_pos == col_pos, ids, 0.0), axis=1, keepdims=True)
    allowed = (row_pos >= col_pos) & (tall == ids)
    seen = rows_of_first(ids)
    before = jnp.where(odd, pick_ids(odd, side[0], side[0]), -1.0) == ids[:, 0:1]
    for pair in range(pairs):
        q_two = q_ref[:, cut(pair)]
        near = attend(q_two, *pick_pair(odd, high, low, pair, rows), allowed)
        earlier = attend(q_two, *pick_pair(odd, side, side, pair, rows), before)
        y_ref[pair * rows : (pair + 1) * rows, :] = near + jnp.where(seen, earlier, 0.0)
    deliver_if(lax.axis_index("ctx") < 2, pairs, y_ref, o_hbm, o_ref, sem)


def finish(y, o_ref, pair):
    low = lower_half(y.shape)
    square = y * y
    sum_low = jnp.sum(jnp.where(low, square, 0.0), axis=1, keepdims=True)
    sum_high = jnp.sum(jnp.where(low, 0.0, square), axis=1, keepdims=True)
    mean = jnp.where(low, sum_low, sum_high) * (1.0 / HW)
    o_ref[:, cut(pair)] = (y * lax.rsqrt(mean + EPS)).astype(o_ref.dtype)


def deliver_if(wanted, pairs, y_ref, o_hbm, o_ref, sem):
    rows = o_ref.shape[0]

    @pl.when(wanted)
    def _():
        for pair in range(pairs):
            finish(y_ref[pair * rows : (pair + 1) * rows, :], o_ref, pair)
        copy = pltpu.make_async_copy(o_ref, o_hbm, sem)
        copy.start()
        copy.wait()


def near_body(pairs, q_ref, own_ref, y_ref, _, *refs):
    (high, low, high_side, low_side), (t_ref, o_hbm, o_ref, sem) = groups_of(refs, 4, pairs)
    rows = q_ref.shape[0]
    odd = is_odd()
    usable = lax.axis_index("ctx") >= 2

    @pl.when(usable)
    def _():
        ids = own_ref[...]
        seen = rows_of_first(ids)
        sources = ((high, low), (low_side, high_side))
        masks = [
            jnp.where(usable, pick_ids(odd, this[0], other[0]), -1.0) == ids[:, 0:1]
            for this, other in sources
        ]
        for pair in range(pairs):
            q_two = q_ref[:, cut(pair)]
            total = jnp.zeros((rows, LANES), jnp.float32)
            for (this, other), mask in zip(sources, masks, strict=True):
                total = total + attend(q_two, *pick_pair(odd, this, other, pair, rows), mask)
            span = slice(pair * rows, (pair + 1) * rows)
            t_ref[span, :] = y_ref[span, :] + jnp.where(seen, total, 0.0)

    here = lax.axis_index("ctx")
    deliver_if((here >= 2) & (here < 4), pairs, t_ref, o_hbm, o_ref, sem)


def far_body(pair, high0, low0, side0, high, low, side, o_ref):
    rows = o_ref.shape[0]
    odd = is_odd()
    here = lax.axis_index("ctx")

    @pl.when((here >= 2) & (here < lax.axis_size("ctx") - 2))
    def _():
        first = pick_ids(odd, low0, high0)[:, 0:1]
        near_mask = pick_ids(odd, high0, low0) == first
        side_mask = jnp.where(odd, -1.0, pick_ids(odd, side0, side0)) == first
        q_two = pick(odd, low0, high0, pair * rows, rows).astype(jnp.bfloat16)
        total = attend(q_two, *pick_pair(odd, [high], [low], 0, rows), near_mask)
        o_ref[...] = total + attend(q_two, *pick_pair(odd, [side], [side], 0, rows), side_mask)


def last_body(pair, own_ref, y_ref, _, high, low, o_hbm, o_ref, sem):
    rows = o_ref.shape[0]
    odd = is_odd()

    @pl.when(lax.axis_index("ctx") >= 4)
    def _():
        seen = rows_of_first(own_ref[...])
        came = pick(odd, high, low, 0, rows)
        y = y_ref[pair * rows : (pair + 1) * rows, :] + jnp.where(seen, came, 0.0)
        finish(y, o_ref, 0)
        copy = pltpu.make_async_copy(o_ref, o_hbm.at[:, cut(pair)], sem)
        copy.start()
        copy.wait()


def call(body, out, flops, *args, **extra):
    moved = sum(a.size * a.dtype.itemsize for a in args)
    return pl.pallas_call(
        body,
        out_shape=out,
        cost_estimate=pl.CostEstimate(flops=flops, bytes_accessed=moved, transcendentals=0),
        compiler_params=pltpu.CompilerParams(vmem_limit_bytes=GRANT),
        **extra,
    )(*args)


def f32(*shape):
    return jax.ShapeDtypeStruct(shape, jnp.float32)


def per_device(queries, keys, values, doc_ids):
    rows, columns = queries.shape
    assert columns % LANES == 0 and rows == LANES and lax.axis_size("ctx") % 2 == 0
    assert MOST <= 4 * rows
    pairs = columns // LANES
    one = 4 * rows * rows * LANES
    ids = doc_ids.reshape(1, rows)
    held = [pltpu.with_memory_space_constraint(x, pltpu.HBM) for x in (keys, values, queries, ids)]
    load = f32(max(2, pairs) * rows + TILE, LANES)
    y_shape = f32(pairs * rows, LANES)
    every = range(pairs)

    def each(moved, arrays):
        out = []
        for pair in every:
            out.append(None if arrays[pair] is None else moved(arrays[pair]))
        return out

    high, low, *rest, own = call(
        functools.partial(pack_body, pairs),
        (load, load, *[f32(2 * rows, LANES)] * (pairs - 1), f32(1, rows)),
        0,
        *held,
        in_specs=[pl.BlockSpec(memory_space=pltpu.HBM)] * 4,
        scratch_shapes=[pltpu.VMEM((rows, columns), x.dtype) for x in (keys, values, queries)]
        + [pltpu.VMEM((1, rows), ids.dtype), pltpu.SemaphoreType.DMA((4,))],
    )
    highs, lows = [high, *rest], [low, *rest]
    got_high = [snake(high, 1, 0)]
    got_low = [snake(low, 0, 0)]
    for pair in range(1, pairs):
        if UP == "S":
            got_high.append(snake(rest[pair - 1], 1, 0))
            got_low.append(snake(rest[pair - 1], 0, 0))
        else:
            got_high.append((climb if UP == "C" else rise)(rest[pair - 1], 0))
            got_low.append(got_high[-1])
    side = each(trade, lows)
    high_side = each(trade, got_high)
    low_side = []
    for pair in every:
        if pair and UP != "S":
            low_side.append(high_side[pair])
        else:
            low_side.append(trade(got_low[pair]))
    lead = (got_high[0], got_low[0], high_side[0])

    def backs(value, kind):
        if kind == "T":
            one_way = snake(value, 1, 1)
            return [one_way, snake(value, 0, 1)]
        return [(climb if kind == "C" else rise)(value, 1)] * 2

    back = []
    if len(BACK) == 1:
        far = call(
            functools.partial(far_all, pairs), y_shape, 4 * pairs * one,
            *got_high, *got_low, *high_side,
        )
        back = backs(far, BACK) * pairs
    else:
        for pair in every:
            args = (*lead, got_high[pair], got_low[pair], high_side[pair])
            body = functools.partial(far_body, pair)
            far = call(body, f32(rows, LANES), 4 * one, *args)
            back += backs(far, BACK[pair])
    out = jax.ShapeDtypeStruct((rows, columns), queries.dtype)
    staged = [pltpu.VMEM(out.shape, out.dtype), pltpu.SemaphoreType.DMA(())]
    here, there = pl.BlockSpec(memory_space=pltpu.VMEM), pl.BlockSpec(memory_space=pltpu.HBM)
    y, partly = call(
        functools.partial(local_body, pairs),
        (y_shape, out),
        4 * pairs * one,
        queries,
        *highs,
        *lows,
        *side,
        out_specs=(here, there),
        scratch_shapes=staged,
    )
    y, partly = call(
        functools.partial(near_body, pairs),
        (y_shape, out),
        4 * pairs * one,
        queries,
        own,
        y,
        partly,
        *got_high,
        *got_low,
        *high_side,
        *low_side,
        in_specs=[here] * 3 + [there] + [here] * (4 * pairs),
        out_specs=(here, there),
        scratch_shapes=staged,
        input_output_aliases={3: 1},
    )
    for pair in every:
        partly = call(
            functools.partial(last_body, pair),
            out,
            0,
            own,
            y,
            partly,
            *back[2 * pair : 2 * pair + 2],
            in_specs=[here, here, there, here, here],
            out_specs=there,
            scratch_shapes=[pltpu.VMEM((rows, LANES), out.dtype), staged[1]],
            input_output_aliases={2: 0},
        )
    return partly


UP = "C"
BACK = "CC"


def solution(mesh):
    placed = P(("groups", "ctx"), ("heads", "rep"))
    return jax.shard_map(
        per_device,
        mesh=mesh,
        in_specs=(placed, placed, placed, P(("groups", "ctx"))),
        out_specs=placed,
        check_vma=False,
    )
```

```python
import functools

import jax
import jax.numpy as jnp
from jax import lax
from jax.experimental import pallas as pl
from jax.experimental.pallas import tpu as pltpu
from jax.sharding import PartitionSpec as P


HW = 64
MOST = 512
LANES = 128
TILE = 8
EPS = 1e-06
GRANT = 16 << 20


def snake(x, rising):
    couples = lax.axis_size("ctx") // 2
    pairs = []
    for couple in range(couples):
        up, down = 2 * couple + rising, 2 * couple + 1 - rising
        pairs.append((up, up + 2 if couple < couples - 1 else down))
        pairs.append((down, down - 2 if couple > 0 else up))
    return lax.ppermute(x, "ctx", pairs)


def climb(x, first, stop):
    pairs = []
    for couple in range(lax.axis_size("ctx") // 2):
        for side in range(2):
            here, stay = 2 * couple + side, not first <= couple < stop or stop - first < 2
            target = couple + 1 if couple + 1 < stop else first
            pairs.append((here, here ^ 1 if stay else 2 * target + side))
    return lax.ppermute(x, "ctx", pairs)


def exchange(x, first):
    couples = lax.axis_size("ctx") // 2
    pairs = []
    for here in range(2 * couples):
        couple = here // 2
        other = couple + 1 if (couple - first) % 2 == 0 else couple - 1
        met = couple >= first and first <= other < couples
        pairs.append((here, 2 * other + here % 2 if met else here ^ 1))
    return lax.ppermute(x, "ctx", pairs)


def trade(x):
    return lax.ppermute(x, "ctx", [(i, i ^ 1) for i in range(lax.axis_size("ctx"))])


def is_odd():
    return lax.axis_index("ctx") % 2 == 1


def lower_half(shape):
    return lax.broadcasted_iota(jnp.int32, shape, 1) % LANES < HW


def two_heads(block):
    low = lower_half(block.shape)
    zero = jnp.zeros_like(block)
    both = jnp.concatenate([jnp.where(low, block, zero), jnp.where(low, zero, block)], axis=0)
    return both.astype(jnp.bfloat16)


def attend(q_two, keys, values, mask):
    scores = lax.dot_general(
        q_two, two_heads(keys), (((1,), (1,)), ((), ())), preferred_element_type=jnp.float32
    )
    mask = jnp.concatenate([mask, mask], axis=1)
    weights = jnp.where(mask, scores * scores, jnp.zeros_like(scores)).astype(jnp.bfloat16)
    return jnp.dot(weights, two_heads(values), preferred_element_type=jnp.float32)


def pick(flag, this, other, start, size):
    return jnp.where(flag, this[start : start + size, :], other[start : start + size, :])


def pick_ids(flag, this, other):
    return pick(flag, this, other, this.shape[0] - TILE, 1)


def pick_pair(flag, these, others, pair, rows):
    this, other = these[pair], others[pair]
    return pick(flag, this, other, 0, rows), pick(flag, this, other, rows, rows)


def rows_of_first(ids):
    count = jnp.sum(jnp.where(ids == ids[:, 0:1], 1.0, 0.0), axis=1, keepdims=True)
    shape = (ids.shape[1], LANES)
    return lax.broadcasted_iota(jnp.int32, shape, 0).astype(jnp.float32) < count


def cut(pair):
    return slice(pair * LANES, (pair + 1) * LANES)


def groups_of(refs, count, pairs):
    return [refs[at * pairs : (at + 1) * pairs] for at in range(count)], refs[count * pairs :]


def pack_body(pairs, k_hbm, v_hbm, q_hbm, ids_hbm, high, low, *refs):
    rest, (own_ref, k_ref, v_ref, q_ref, ids_ref, sem) = refs[: pairs - 1], refs[pairs - 1 :]
    rows = k_ref.shape[0]
    moves = []
    routes = [(k_hbm, k_ref), (v_hbm, v_ref), (q_hbm, q_ref), (ids_hbm, ids_ref)]
    for at, (source, target) in enumerate(routes):
        moves.append(pltpu.make_async_copy(source, target, sem.at[at]))
        moves[-1].start()
    for item in moves:
        item.wait()
    ids = ids_ref[...].astype(jnp.float32)
    own_ref[...] = ids
    wide = jnp.broadcast_to(ids, (TILE, rows))
    odd = is_odd()

    def put(target, pair):
        target[:rows, :] = k_ref[:, cut(pair)].astype(jnp.float32)
        target[rows : 2 * rows, :] = v_ref[:, cut(pair)].astype(jnp.float32)

    def fill(up, down):
        size = up.shape[0] - TILE
        put(up, 0)
        for pair in range(pairs):
            down[pair * rows : (pair + 1) * rows, :] = q_ref[:, cut(pair)].astype(jnp.float32)
        for target, done in ((up, 2 * rows), (down, pairs * rows)):
            if done < size:
                target[done:size, :] = jnp.zeros((size - done, LANES), jnp.float32)
            target[size:, :] = wide

    @pl.when(odd)
    def _():
        fill(high, low)

    @pl.when(jnp.logical_not(odd))
    def _():
        fill(low, high)

    for pair in range(1, pairs):
        put(rest[pair - 1], pair)


def local_body(pairs, q_ref, *refs):
    (high, low, side), (y_ref, o_hbm, o_ref, sem) = groups_of(refs, 3, pairs)
    rows = q_ref.shape[0]
    odd = is_odd()
    ids = pick_ids(odd, high[0], low[0])
    row_pos = lax.broadcasted_iota(jnp.int32, (rows, rows), 0)
    col_pos = lax.broadcasted_iota(jnp.int32, (rows, rows), 1)
    tall = jnp.sum(jnp.where(row_pos == col_pos, ids, 0.0), axis=1, keepdims=True)
    allowed = (row_pos >= col_pos) & (tall == ids)
    seen = rows_of_first(ids)
    before = jnp.where(odd, pick_ids(odd, side[0], side[0]), -1.0) == ids[:, 0:1]
    for pair in range(pairs):
        q_two = q_ref[:, cut(pair)]
        near = attend(q_two, *pick_pair(odd, high, low, pair, rows), allowed)
        earlier = attend(q_two, *pick_pair(odd, side, side, pair, rows), before)
        y_ref[pair * rows : (pair + 1) * rows, :] = near + jnp.where(seen, earlier, 0.0)
    deliver_if(lax.axis_index("ctx") < 2, pairs, y_ref, o_hbm, o_ref, sem)


def finish(y, o_ref, pair):
    low = lower_half(y.shape)
    square = y * y
    sum_low = jnp.sum(jnp.where(low, square, 0.0), axis=1, keepdims=True)
    sum_high = jnp.sum(jnp.where(low, 0.0, square), axis=1, keepdims=True)
    mean = jnp.where(low, sum_low, sum_high) * (1.0 / HW)
    o_ref[:, cut(pair)] = (y * lax.rsqrt(mean + EPS)).astype(o_ref.dtype)


def deliver_if(wanted, pairs, y_ref, o_hbm, o_ref, sem):
    rows = o_ref.shape[0]

    @pl.when(wanted)
    def _():
        for pair in range(pairs):
            finish(y_ref[pair * rows : (pair + 1) * rows, :], o_ref, pair)
        copy = pltpu.make_async_copy(o_ref, o_hbm, sem)
        copy.start()
        copy.wait()


def near_body(stop, pairs, q_ref, own_ref, y_ref, _, *refs):
    (high, low, high_side, low_side), (t_ref, o_hbm, o_ref, sem) = groups_of(refs, 4, pairs)
    rows = q_ref.shape[0]
    odd = is_odd()
    usable = lax.axis_index("ctx") >= 2

    @pl.when(usable)
    def _():
        ids = own_ref[...]
        seen = rows_of_first(ids)
        sources = ((high, low), (low_side, high_side))
        masks = [
            jnp.where(usable, pick_ids(odd, this[0], other[0]), -1.0) == ids[:, 0:1]
            for this, other in sources
        ]
        below = lax.axis_index("ctx") < 2 * stop
        for pair in range(pairs):
            q_two = q_ref[:, cut(pair)]
            total = jnp.zeros((rows, LANES), jnp.float32)
            for (this, other), mask in zip(sources, masks, strict=True):
                mask = mask if pair == 0 else mask & below
                total = total + attend(q_two, *pick_pair(odd, this, other, pair, rows), mask)
            span = slice(pair * rows, (pair + 1) * rows)
            t_ref[span, :] = y_ref[span, :] + jnp.where(seen, total, 0.0)

    here = lax.axis_index("ctx")
    deliver_if((here >= 2) & (here < 4), pairs, t_ref, o_hbm, o_ref, sem)


def top_body(stop, pair, high0, low0, own_ref, side0, mine, side, o_ref):
    rows = o_ref.shape[0]
    odd = is_odd()

    @pl.when(lax.axis_index("ctx") // 2 == stop - 1)
    def _():
        first = pick_ids(odd, low0, high0)[:, 0:1]
        q_two = pick(odd, low0, high0, pair * rows, rows).astype(jnp.bfloat16)
        total = attend(q_two, mine[:rows, :], mine[rows : 2 * rows, :], own_ref[...] == first)
        mask = pick_ids(odd, side0, side0) == first
        o_ref[...] = total + attend(q_two, side[:rows, :], side[rows : 2 * rows, :], mask)


def far_body(stop, pair, high0, low0, side0, high, low, side, *refs):
    o_ref = refs[-1]
    rows = o_ref.shape[0]
    odd = is_odd()
    here = lax.axis_index("ctx")

    @pl.when((here >= 2) & (here < lax.axis_size("ctx") - 2))
    def _():
        first = pick_ids(odd, low0, high0)[:, 0:1]
        near_mask = pick_ids(odd, high0, low0) == first
        side_mask = jnp.where(odd, -1.0, pick_ids(odd, side0, side0)) == first
        q_two = pick(odd, low0, high0, pair * rows, rows).astype(jnp.bfloat16)
        total = attend(q_two, *pick_pair(odd, [high], [low], 0, rows), near_mask)
        total = total + attend(q_two, *pick_pair(odd, [side], [side], 0, rows), side_mask)
        if len(refs) > 1:
            total = total + jnp.where(here // 2 == stop - 1, refs[0][...], 0.0)
        o_ref[...] = total


def last_body(pair, parity, own_ref, y_ref, _, came, o_hbm, o_ref, sem):
    rows = o_ref.shape[0]
    couple = lax.axis_index("ctx") // 2
    wanted = couple >= 2
    if parity is not None:
        wanted = wanted & (couple % 2 == parity)

    @pl.when(wanted)
    def _():
        seen = rows_of_first(own_ref[...])
        y = y_ref[pair * rows : (pair + 1) * rows, :] + jnp.where(seen, came[...], 0.0)
        finish(y, o_ref, 0)
        copy = pltpu.make_async_copy(o_ref, o_hbm.at[:, cut(pair)], sem)
        copy.start()
        copy.wait()


def call(body, out, flops, *args, **extra):
    moved = sum(a.size * a.dtype.itemsize for a in args)
    return pl.pallas_call(
        body,
        out_shape=out,
        cost_estimate=pl.CostEstimate(flops=flops, bytes_accessed=moved, transcendentals=0),
        compiler_params=pltpu.CompilerParams(vmem_limit_bytes=GRANT),
        **extra,
    )(*args)


def f32(*shape):
    return jax.ShapeDtypeStruct(shape, jnp.float32)


def per_device(queries, keys, values, doc_ids):
    rows, columns = queries.shape
    assert columns % LANES == 0 and rows == LANES and lax.axis_size("ctx") % 2 == 0
    assert MOST <= 4 * rows
    pairs = columns // LANES
    one = 4 * rows * rows * LANES
    ids = doc_ids.reshape(1, rows)
    held = [pltpu.with_memory_space_constraint(x, pltpu.HBM) for x in (keys, values, queries, ids)]
    load = f32(max(2, pairs) * rows + TILE, LANES)
    y_shape = f32(pairs * rows, LANES)
    every = range(pairs)
    couples = lax.axis_size("ctx") // 2
    stop = couples - 1 if couples > 2 else couples

    def each(moved, arrays):
        out = []
        for pair in every:
            out.append(None if arrays[pair] is None else moved(arrays[pair]))
        return out

    high, low, *rest, own = call(
        functools.partial(pack_body, pairs),
        (load, load, *[f32(2 * rows, LANES)] * (pairs - 1), f32(1, rows)),
        0,
        *held,
        in_specs=[pl.BlockSpec(memory_space=pltpu.HBM)] * 4,
        scratch_shapes=[pltpu.VMEM((rows, columns), x.dtype) for x in (keys, values, queries)]
        + [pltpu.VMEM((1, rows), ids.dtype), pltpu.SemaphoreType.DMA((4,))],
    )
    highs, lows = [high, *rest], [low, *rest]
    got_high = [snake(high, 1)]
    got_low = [snake(low, 0)]
    got = each(lambda x: climb(x, 0, stop), [None, *rest])[1:]
    got_high, got_low = got_high + got, got_low + got
    side = each(trade, lows)
    high_side = each(trade, got_high)
    low_side = [trade(got_low[0]), *high_side[1:]]
    lead = (got_high[0], got_low[0])
    back = []
    for pair in every:
        extra = []
        if pair and stop < couples:
            args = (*lead, own, side[0], rest[pair - 1], side[pair])
            body = functools.partial(top_body, stop, pair)
            extra = [call(body, f32(rows, LANES), 4 * one, *args)]
        args = (*lead, high_side[0], got_high[pair], got_low[pair], high_side[pair], *extra)
        body = functools.partial(far_body, stop, pair)
        far = call(body, f32(rows, LANES), 4 * one, *args)
        if pair < pairs - 1:
            back.append([(None, climb(far, 1, couples))])
        else:
            evens = exchange(far, 1)
            back.append([(0, evens), (1, exchange(far, 2))])
    out = jax.ShapeDtypeStruct((rows, columns), queries.dtype)
    staged = [pltpu.VMEM(out.shape, out.dtype), pltpu.SemaphoreType.DMA(())]
    here, there = pl.BlockSpec(memory_space=pltpu.VMEM), pl.BlockSpec(memory_space=pltpu.HBM)
    y, partly = call(
        functools.partial(local_body, pairs),
        (y_shape, out),
        4 * pairs * one,
        queries,
        *highs,
        *lows,
        *side,
        out_specs=(here, there),
        scratch_shapes=staged,
    )
    y, partly = call(
        functools.partial(near_body, stop, pairs),
        (y_shape, out),
        4 * pairs * one,
        queries,
        own,
        y,
        partly,
        *got_high,
        *got_low,
        *high_side,
        *low_side,
        in_specs=[here] * 3 + [there] + [here] * (4 * pairs),
        out_specs=(here, there),
        scratch_shapes=staged,
        input_output_aliases={3: 1},
    )
    for pair in every:
        for parity, came in back[pair]:
            partly = call(
                functools.partial(last_body, pair, parity),
                out,
                0,
                own,
                y,
                partly,
                came,
                in_specs=[here, here, there, here],
                out_specs=there,
                scratch_shapes=[pltpu.VMEM((rows, LANES), out.dtype), staged[1]],
                input_output_aliases={2: 0},
            )
    return partly


def solution(mesh):
    placed = P(("groups", "ctx"), ("heads", "rep"))
    return jax.shard_map(
        per_device,
        mesh=mesh,
        in_specs=(placed, placed, placed, P(("groups", "ctx"))),
        out_specs=placed,
        check_vma=False,
    )
```

```python
import functools

import jax
import jax.numpy as jnp
from jax import lax
from jax.experimental import pallas as pl
from jax.experimental.pallas import tpu as pltpu
from jax.sharding import PartitionSpec as P


HW = 64
MOST = 512
LANES = 128
TILE = 8
EPS = 1e-06
GRANT = 16 << 20


def snake(x, rising):
    couples = lax.axis_size("ctx") // 2
    pairs = []
    for couple in range(couples):
        up, down = 2 * couple + rising, 2 * couple + 1 - rising
        pairs.append((up, up + 2 if couple < couples - 1 else down))
        pairs.append((down, down - 2 if couple > 0 else up))
    return lax.ppermute(x, "ctx", pairs)


def climb(x, first, stop):
    pairs = []
    for couple in range(lax.axis_size("ctx") // 2):
        for side in range(2):
            here, stay = 2 * couple + side, not first <= couple < stop or stop - first < 2
            target = couple + 1 if couple + 1 < stop else first
            pairs.append((here, here ^ 1 if stay else 2 * target + side))
    return lax.ppermute(x, "ctx", pairs)


def exchange(x, first):
    couples = lax.axis_size("ctx") // 2
    pairs = []
    for here in range(2 * couples):
        couple = here // 2
        other = couple + 1 if (couple - first) % 2 == 0 else couple - 1
        met = couple >= first and first <= other < couples
        pairs.append((here, 2 * other + here % 2 if met else here ^ 1))
    return lax.ppermute(x, "ctx", pairs)


def trade(x):
    return lax.ppermute(x, "ctx", [(i, i ^ 1) for i in range(lax.axis_size("ctx"))])


def is_odd():
    return lax.axis_index("ctx") % 2 == 1


def lower_half(shape):
    return lax.broadcasted_iota(jnp.int32, shape, 1) % LANES < HW


def two_heads(block):
    low = lower_half(block.shape)
    zero = jnp.zeros_like(block)
    both = jnp.concatenate([jnp.where(low, block, zero), jnp.where(low, zero, block)], axis=0)
    return both.astype(jnp.bfloat16)


def attend(q_two, keys, values, mask):
    scores = lax.dot_general(
        q_two, two_heads(keys), (((1,), (1,)), ((), ())), preferred_element_type=jnp.float32
    )
    mask = jnp.concatenate([mask, mask], axis=1)
    weights = jnp.where(mask, scores * scores, jnp.zeros_like(scores)).astype(jnp.bfloat16)
    return jnp.dot(weights, two_heads(values), preferred_element_type=jnp.float32)


def pick(flag, this, other, start, size):
    return jnp.where(flag, this[start : start + size, :], other[start : start + size, :])


def pick_ids(flag, this, other):
    return pick(flag, this, other, this.shape[0] - TILE, 1)


def pick_pair(flag, these, others, pair, rows):
    this, other = these[pair], others[pair]
    return pick(flag, this, other, 0, rows), pick(flag, this, other, rows, rows)


def rows_of_first(ids):
    count = jnp.sum(jnp.where(ids == ids[:, 0:1], 1.0, 0.0), axis=1, keepdims=True)
    shape = (ids.shape[1], LANES)
    return lax.broadcasted_iota(jnp.int32, shape, 0).astype(jnp.float32) < count


def cut(pair):
    return slice(pair * LANES, (pair + 1) * LANES)


def groups_of(refs, count, pairs):
    return [refs[at * pairs : (at + 1) * pairs] for at in range(count)], refs[count * pairs :]


def pack_body(pairs, k_hbm, v_hbm, q_hbm, ids_hbm, high, low, *refs):
    rest, (own_ref, k_ref, v_ref, q_ref, ids_ref, sem) = refs[: pairs - 1], refs[pairs - 1 :]
    rows = k_ref.shape[0]
    moves = []
    routes = [(k_hbm, k_ref), (v_hbm, v_ref), (q_hbm, q_ref), (ids_hbm, ids_ref)]
    for at, (source, target) in enumerate(routes):
        moves.append(pltpu.make_async_copy(source, target, sem.at[at]))
        moves[-1].start()
    odd = is_odd()
    size = high.shape[0] - TILE

    def each_side(put):
        @pl.when(odd)
        def _():
            put(high, low)

        @pl.when(jnp.logical_not(odd))
        def _():
            put(low, high)

    moves[0].wait()
    moves[1].wait()

    def put_up(up, _):
        up[:rows, :] = k_ref[:, cut(0)].astype(jnp.float32)
        up[rows : 2 * rows, :] = v_ref[:, cut(0)].astype(jnp.float32)
        if 2 * rows < size:
            up[2 * rows : size, :] = jnp.zeros((size - 2 * rows, LANES), jnp.float32)

    each_side(put_up)
    for pair in range(1, pairs):
        rest[pair - 1][:rows, :] = k_ref[:, cut(pair)].astype(jnp.float32)
        rest[pair - 1][rows : 2 * rows, :] = v_ref[:, cut(pair)].astype(jnp.float32)
    moves[2].wait()

    def put_down(_, down):
        for pair in range(pairs):
            down[pair * rows : (pair + 1) * rows, :] = q_ref[:, cut(pair)].astype(jnp.float32)
        if pairs * rows < size:
            down[pairs * rows : size, :] = jnp.zeros((size - pairs * rows, LANES), jnp.float32)

    each_side(put_down)
    moves[3].wait()
    ids = ids_ref[...].astype(jnp.float32)
    own_ref[...] = ids
    wide = jnp.broadcast_to(ids, (TILE, rows))
    high[size:, :] = wide
    low[size:, :] = wide


def local_body(pairs, q_ref, *refs):
    (high, low, side), (y_ref, o_hbm, o_ref, sem) = groups_of(refs, 3, pairs)
    rows = q_ref.shape[0]
    odd = is_odd()
    ids = pick_ids(odd, high[0], low[0])
    row_pos = lax.broadcasted_iota(jnp.int32, (rows, rows), 0)
    col_pos = lax.broadcasted_iota(jnp.int32, (rows, rows), 1)
    tall = jnp.sum(jnp.where(row_pos == col_pos, ids, 0.0), axis=1, keepdims=True)
    allowed = (row_pos >= col_pos) & (tall == ids)
    seen = rows_of_first(ids)
    before = jnp.where(odd, pick_ids(odd, side[0], side[0]), -1.0) == ids[:, 0:1]
    for pair in range(pairs):
        q_two = q_ref[:, cut(pair)]
        near = attend(q_two, *pick_pair(odd, high, low, pair, rows), allowed)
        earlier = attend(q_two, *pick_pair(odd, side, side, pair, rows), before)
        y_ref[pair * rows : (pair + 1) * rows, :] = near + jnp.where(seen, earlier, 0.0)
    deliver_if(lax.axis_index("ctx") < 2, pairs, y_ref, o_hbm, o_ref, sem)


def finish(y, o_ref, pair):
    low = lower_half(y.shape)
    square = y * y
    sum_low = jnp.sum(jnp.where(low, square, 0.0), axis=1, keepdims=True)
    sum_high = jnp.sum(jnp.where(low, 0.0, square), axis=1, keepdims=True)
    mean = jnp.where(low, sum_low, sum_high) * (1.0 / HW)
    o_ref[:, cut(pair)] = (y * lax.rsqrt(mean + EPS)).astype(o_ref.dtype)


def deliver_if(wanted, pairs, y_ref, o_hbm, o_ref, sem):
    rows = o_ref.shape[0]

    @pl.when(wanted)
    def _():
        for pair in range(pairs):
            finish(y_ref[pair * rows : (pair + 1) * rows, :], o_ref, pair)
        copy = pltpu.make_async_copy(o_ref, o_hbm, sem)
        copy.start()
        copy.wait()


def near_body(stop, pairs, q_ref, own_ref, y_ref, _, *refs):
    (high, low, high_side, low_side), (t_ref, o_hbm, o_ref, sem) = groups_of(refs, 4, pairs)
    rows = q_ref.shape[0]
    odd = is_odd()
    usable = lax.axis_index("ctx") >= 2

    @pl.when(usable)
    def _():
        ids = own_ref[...]
        seen = rows_of_first(ids)
        sources = ((high, low), (low_side, high_side))
        masks = [
            jnp.where(usable, pick_ids(odd, this[0], other[0]), -1.0) == ids[:, 0:1]
            for this, other in sources
        ]
        below = lax.axis_index("ctx") < 2 * stop
        for pair in range(pairs):
            q_two = q_ref[:, cut(pair)]
            total = jnp.zeros((rows, LANES), jnp.float32)
            for (this, other), mask in zip(sources, masks, strict=True):
                mask = mask if pair == 0 else mask & below
                total = total + attend(q_two, *pick_pair(odd, this, other, pair, rows), mask)
            span = slice(pair * rows, (pair + 1) * rows)
            t_ref[span, :] = y_ref[span, :] + jnp.where(seen, total, 0.0)

    here = lax.axis_index("ctx")
    deliver_if((here >= 2) & (here < 4), pairs, t_ref, o_hbm, o_ref, sem)


def top_body(stop, pair, high0, low0, own_ref, side0, mine, side, o_ref):
    rows = o_ref.shape[0]
    odd = is_odd()

    @pl.when(lax.axis_index("ctx") // 2 == stop - 1)
    def _():
        first = pick_ids(odd, low0, high0)[:, 0:1]
        q_two = pick(odd, low0, high0, pair * rows, rows).astype(jnp.bfloat16)
        total = attend(q_two, mine[:rows, :], mine[rows : 2 * rows, :], own_ref[...] == first)
        mask = pick_ids(odd, side0, side0) == first
        o_ref[...] = total + attend(q_two, side[:rows, :], side[rows : 2 * rows, :], mask)


def far_body(stop, pair, high0, low0, side0, high, low, side, *refs):
    o_ref = refs[-1]
    rows = o_ref.shape[0]
    odd = is_odd()
    here = lax.axis_index("ctx")

    @pl.when((here >= 2) & (here < lax.axis_size("ctx") - 2))
    def _():
        first = pick_ids(odd, low0, high0)[:, 0:1]
        near_mask = pick_ids(odd, high0, low0) == first
        side_mask = jnp.where(odd, -1.0, pick_ids(odd, side0, side0)) == first
        q_two = pick(odd, low0, high0, pair * rows, rows).astype(jnp.bfloat16)
        total = attend(q_two, *pick_pair(odd, [high], [low], 0, rows), near_mask)
        total = total + attend(q_two, *pick_pair(odd, [side], [side], 0, rows), side_mask)
        if len(refs) > 1:
            total = total + jnp.where(here // 2 == stop - 1, refs[0][...], 0.0)
        o_ref[...] = total


def last_body(pair, parity, own_ref, y_ref, _, came, o_hbm, o_ref, sem):
    rows = o_ref.shape[0]
    couple = lax.axis_index("ctx") // 2
    wanted = couple >= 2
    if parity is not None:
        wanted = wanted & (couple % 2 == parity)

    @pl.when(wanted)
    def _():
        seen = rows_of_first(own_ref[...])
        y = y_ref[pair * rows : (pair + 1) * rows, :] + jnp.where(seen, came[...], 0.0)
        finish(y, o_ref, 0)
        copy = pltpu.make_async_copy(o_ref, o_hbm.at[:, cut(pair)], sem)
        copy.start()
        copy.wait()


def call(body, out, flops, *args, **extra):
    moved = sum(a.size * a.dtype.itemsize for a in args)
    return pl.pallas_call(
        body,
        out_shape=out,
        cost_estimate=pl.CostEstimate(flops=flops, bytes_accessed=moved, transcendentals=0),
        compiler_params=pltpu.CompilerParams(vmem_limit_bytes=GRANT),
        **extra,
    )(*args)


def f32(*shape):
    return jax.ShapeDtypeStruct(shape, jnp.float32)


def per_device(queries, keys, values, doc_ids):
    rows, columns = queries.shape
    assert columns % LANES == 0 and rows == LANES and lax.axis_size("ctx") % 2 == 0
    assert MOST <= 4 * rows
    pairs = columns // LANES
    one = 4 * rows * rows * LANES
    ids = doc_ids.reshape(1, rows)
    held = [pltpu.with_memory_space_constraint(x, pltpu.HBM) for x in (keys, values, queries, ids)]
    load = f32(max(2, pairs) * rows + TILE, LANES)
    y_shape = f32(pairs * rows, LANES)
    every = range(pairs)
    couples = lax.axis_size("ctx") // 2
    stop = couples - 1 if couples > 2 else couples

    def each(moved, arrays):
        out = []
        for pair in every:
            out.append(None if arrays[pair] is None else moved(arrays[pair]))
        return out

    high, low, *rest, own = call(
        functools.partial(pack_body, pairs),
        (load, load, *[f32(2 * rows, LANES)] * (pairs - 1), f32(1, rows)),
        0,
        *held,
        in_specs=[pl.BlockSpec(memory_space=pltpu.HBM)] * 4,
        scratch_shapes=[pltpu.VMEM((rows, columns), x.dtype) for x in (keys, values, queries)]
        + [pltpu.VMEM((1, rows), ids.dtype), pltpu.SemaphoreType.DMA((4,))],
    )
    highs, lows = [high, *rest], [low, *rest]
    got_high = [snake(high, 1)]
    got_low = [snake(low, 0)]
    got = each(lambda x: climb(x, 0, stop), [None, *rest])[1:]
    got_high, got_low = got_high + got, got_low + got
    side = each(trade, lows)
    high_side = each(trade, got_high)
    low_side = [trade(got_low[0]), *high_side[1:]]
    lead = (got_high[0], got_low[0])
    back = []
    for pair in every:
        extra = []
        if pair and stop < couples:
            args = (*lead, own, side[0], rest[pair - 1], side[pair])
            body = functools.partial(top_body, stop, pair)
            extra = [call(body, f32(rows, LANES), 4 * one, *args)]
        args = (*lead, high_side[0], got_high[pair], got_low[pair], high_side[pair], *extra)
        body = functools.partial(far_body, stop, pair)
        far = call(body, f32(rows, LANES), 4 * one, *args)
        if pair < pairs - 1:
            back.append([(None, climb(far, 1, couples))])
        else:
            evens = exchange(far, 1)
            back.append([(0, evens), (1, exchange(far, 2))])
    out = jax.ShapeDtypeStruct((rows, columns), queries.dtype)
    staged = [pltpu.VMEM(out.shape, out.dtype), pltpu.SemaphoreType.DMA(())]
    here, there = pl.BlockSpec(memory_space=pltpu.VMEM), pl.BlockSpec(memory_space=pltpu.HBM)
    y, partly = call(
        functools.partial(local_body, pairs),
        (y_shape, out),
        4 * pairs * one,
        queries,
        *highs,
        *lows,
        *side,
        out_specs=(here, there),
        scratch_shapes=staged,
    )
    y, partly = call(
        functools.partial(near_body, stop, pairs),
        (y_shape, out),
        4 * pairs * one,
        queries,
        own,
        y,
        partly,
        *got_high,
        *got_low,
        *high_side,
        *low_side,
        in_specs=[here] * 3 + [there] + [here] * (4 * pairs),
        out_specs=(here, there),
        scratch_shapes=staged,
        input_output_aliases={3: 1},
    )
    for pair in every:
        for parity, came in back[pair]:
            partly = call(
                functools.partial(last_body, pair, parity),
                out,
                0,
                own,
                y,
                partly,
                came,
                in_specs=[here, here, there, here],
                out_specs=there,
                scratch_shapes=[pltpu.VMEM((rows, LANES), out.dtype), staged[1]],
                input_output_aliases={2: 0},
            )
    return partly


def solution(mesh):
    placed = P(("groups", "ctx"), ("heads", "rep"))
    return jax.shard_map(
        per_device,
        mesh=mesh,
        in_specs=(placed, placed, placed, P(("groups", "ctx"))),
        out_specs=placed,
        check_vma=False,
    )
```

```python
import functools

import jax
import jax.numpy as jnp
from jax import lax
from jax.experimental import pallas as pl
from jax.experimental.pallas import tpu as pltpu
from jax.sharding import PartitionSpec as P


HW = 64
MOST = 512
LANES = 128
TILE = 8
EPS = 1e-06
GRANT = 16 << 20


def snake(x, rising, first):
    couples = lax.axis_size("ctx") // 2
    pairs = []
    for couple in range(couples):
        up, down = 2 * couple + rising, 2 * couple + 1 - rising
        pairs.append((up, up + 2 if first <= couple < couples - 1 else down))
        pairs.append((down, down - 2 if couple > first else up))
    return lax.ppermute(x, "ctx", pairs)


def climb(x, first, stop):
    pairs = []
    for couple in range(lax.axis_size("ctx") // 2):
        for side in range(2):
            here, stay = 2 * couple + side, not first <= couple < stop or stop - first < 2
            target = couple + 1 if couple + 1 < stop else first
            pairs.append((here, here ^ 1 if stay else 2 * target + side))
    return lax.ppermute(x, "ctx", pairs)


def exchange(x, first):
    couples = lax.axis_size("ctx") // 2
    pairs = []
    for here in range(2 * couples):
        couple = here // 2
        other = couple + 1 if (couple - first) % 2 == 0 else couple - 1
        met = couple >= first and first <= other < couples
        pairs.append((here, 2 * other + here % 2 if met else here ^ 1))
    return lax.ppermute(x, "ctx", pairs)


def trade(x):
    return lax.ppermute(x, "ctx", [(i, i ^ 1) for i in range(lax.axis_size("ctx"))])


def is_odd():
    return lax.axis_index("ctx") % 2 == 1


def lower_half(shape):
    return lax.broadcasted_iota(jnp.int32, shape, 1) % LANES < HW


def attend(q_two, blocks):
    rows = q_two.shape[0]
    low = lower_half(q_two.shape)
    zero = jnp.zeros_like(q_two)
    stacked = jnp.concatenate([jnp.where(low, q_two, zero), jnp.where(low, zero, q_two)], axis=0)
    keys = jnp.concatenate([block[0].astype(jnp.bfloat16) for block in blocks], axis=0)
    values = jnp.concatenate([block[1].astype(jnp.bfloat16) for block in blocks], axis=0)
    masks = [jnp.broadcast_to(mask, (rows, mask.shape[1])) for _, _, mask in blocks]
    mask = jnp.concatenate(masks, axis=1)
    mask = jnp.concatenate([mask, mask], axis=0)
    scores = lax.dot_general(
        stacked, keys, (((1,), (1,)), ((), ())), preferred_element_type=jnp.float32
    )
    weights = jnp.where(mask, scores * scores, jnp.zeros_like(scores)).astype(jnp.bfloat16)
    both = jnp.dot(weights, values, preferred_element_type=jnp.float32)
    return jnp.where(low, both[:rows, :], both[rows:, :])


def pick(flag, this, other, start, size):
    return jnp.where(flag, this[start : start + size, :], other[start : start + size, :])


def pick_ids(flag, this, other):
    return pick(flag, this, other, this.shape[0] - TILE, 1)


def pick_pair(flag, these, others, pair, rows):
    this, other = these[pair], others[pair]
    return pick(flag, this, other, 0, rows), pick(flag, this, other, rows, rows)


def rows_of_first(ids):
    count = jnp.sum(jnp.where(ids == ids[:, 0:1], 1.0, 0.0), axis=1, keepdims=True)
    shape = (ids.shape[1], LANES)
    return lax.broadcasted_iota(jnp.int32, shape, 0).astype(jnp.float32) < count


def cut(pair):
    return slice(pair * LANES, (pair + 1) * LANES)


def groups_of(refs, count, pairs):
    return [refs[at * pairs : (at + 1) * pairs] for at in range(count)], refs[count * pairs :]


def pack_body(pairs, k_hbm, v_hbm, q_hbm, ids_hbm, high, low, *refs):
    rest, (own_ref, k_ref, v_ref, q_ref, ids_ref, sem) = refs[: pairs - 1], refs[pairs - 1 :]
    rows = k_ref.shape[0]
    moves = []
    routes = [(k_hbm, k_ref), (v_hbm, v_ref), (q_hbm, q_ref), (ids_hbm, ids_ref)]
    for at, (source, target) in enumerate(routes):
        moves.append(pltpu.make_async_copy(source, target, sem.at[at]))
        moves[-1].start()
    for item in moves:
        item.wait()
    ids = ids_ref[...].astype(jnp.float32)
    own_ref[...] = ids
    wide = jnp.broadcast_to(ids, (TILE, rows))
    odd = is_odd()

    def put(target, pair):
        target[:rows, :] = k_ref[:, cut(pair)].astype(jnp.float32)
        target[rows : 2 * rows, :] = v_ref[:, cut(pair)].astype(jnp.float32)

    def fill(up, down):
        size = up.shape[0] - TILE
        put(up, 0)
        for pair in range(pairs):
            down[pair * rows : (pair + 1) * rows, :] = q_ref[:, cut(pair)].astype(jnp.float32)
        for target, done in ((up, 2 * rows), (down, pairs * rows)):
            if done < size:
                target[done:size, :] = jnp.zeros((size - done, LANES), jnp.float32)
            target[size:, :] = wide

    @pl.when(odd)
    def _():
        fill(high, low)

    @pl.when(jnp.logical_not(odd))
    def _():
        fill(low, high)

    for pair in range(1, pairs):
        put(rest[pair - 1], pair)


def local_body(pairs, q_ref, *refs):
    (high, low, side), (y_ref, o_hbm, o_ref, sem) = groups_of(refs, 3, pairs)
    rows = q_ref.shape[0]
    odd = is_odd()
    ids = pick_ids(odd, high[0], low[0])
    row_pos = lax.broadcasted_iota(jnp.int32, (rows, rows), 0)
    col_pos = lax.broadcasted_iota(jnp.int32, (rows, rows), 1)
    tall = jnp.sum(jnp.where(row_pos == col_pos, ids, 0.0), axis=1, keepdims=True)
    allowed = (row_pos >= col_pos) & (tall == ids)
    seen = rows_of_first(ids)
    before = jnp.where(odd, pick_ids(odd, side[0], side[0]), -1.0) == ids[:, 0:1]
    for pair in range(pairs):
        q_two = q_ref[:, cut(pair)]
        mine = (*pick_pair(odd, high, low, pair, rows), allowed)
        earlier = (*pick_pair(odd, side, side, pair, rows), before & seen)
        y_ref[pair * rows : (pair + 1) * rows, :] = attend(q_two, [mine, earlier])
    deliver_if(lax.axis_index("ctx") < 2, pairs, y_ref, o_hbm, o_ref, sem)


def finish(y, o_ref, pair):
    low = lower_half(y.shape)
    square = y * y
    sum_low = jnp.sum(jnp.where(low, square, 0.0), axis=1, keepdims=True)
    sum_high = jnp.sum(jnp.where(low, 0.0, square), axis=1, keepdims=True)
    mean = jnp.where(low, sum_low, sum_high) * (1.0 / HW)
    o_ref[:, cut(pair)] = (y * lax.rsqrt(mean + EPS)).astype(o_ref.dtype)


def deliver_if(wanted, pairs, y_ref, o_hbm, o_ref, sem):
    rows = o_ref.shape[0]

    @pl.when(wanted)
    def _():
        for pair in range(pairs):
            finish(y_ref[pair * rows : (pair + 1) * rows, :], o_ref, pair)
        copy = pltpu.make_async_copy(o_ref, o_hbm, sem)
        copy.start()
        copy.wait()


def near_body(stop, pairs, q_ref, own_ref, y_ref, _, *refs):
    (high, low, high_side, low_side), (t_ref, o_hbm, o_ref, sem) = groups_of(refs, 4, pairs)
    rows = q_ref.shape[0]
    odd = is_odd()
    usable = lax.axis_index("ctx") >= 2

    @pl.when(usable)
    def _():
        ids = own_ref[...]
        seen = rows_of_first(ids)
        sources = ((high, low), (low_side, high_side))
        masks = [
            jnp.where(usable, pick_ids(odd, this[0], other[0]), -1.0) == ids[:, 0:1]
            for this, other in sources
        ]
        below = lax.axis_index("ctx") < 2 * stop
        for pair in range(pairs):
            q_two = q_ref[:, cut(pair)]
            blocks = []
            for (this, other), mask in zip(sources, masks, strict=True):
                mask = mask if pair == 0 else mask & below
                blocks.append((*pick_pair(odd, this, other, pair, rows), mask))
            total = attend(q_two, blocks)
            span = slice(pair * rows, (pair + 1) * rows)
            t_ref[span, :] = y_ref[span, :] + jnp.where(seen, total, 0.0)

    here = lax.axis_index("ctx")
    deliver_if((here >= 2) & (here < 4), pairs, t_ref, o_hbm, o_ref, sem)


def top_body(stop, pair, high0, low0, own_ref, side0, mine, side, o_ref):
    rows = o_ref.shape[0]
    odd = is_odd()

    @pl.when(lax.axis_index("ctx") // 2 == stop - 1)
    def _():
        first = pick_ids(odd, low0, high0)[:, 0:1]
        q_two = pick(odd, low0, high0, pair * rows, rows).astype(jnp.bfloat16)
        blocks = [
            (mine[:rows, :], mine[rows : 2 * rows, :], own_ref[...] == first),
            (side[:rows, :], side[rows : 2 * rows, :], pick_ids(odd, side0, side0) == first),
        ]
        o_ref[...] = attend(q_two, blocks)


def far_body(stop, pair, high0, low0, side0, high, low, side, *refs):
    o_ref = refs[-1]
    rows = o_ref.shape[0]
    odd = is_odd()
    here = lax.axis_index("ctx")

    @pl.when((here >= 2) & (here < lax.axis_size("ctx") - 2))
    def _():
        first = pick_ids(odd, low0, high0)[:, 0:1]
        near_mask = pick_ids(odd, high0, low0) == first
        side_mask = jnp.where(odd, -1.0, pick_ids(odd, side0, side0)) == first
        q_two = pick(odd, low0, high0, pair * rows, rows).astype(jnp.bfloat16)
        blocks = [
            (*pick_pair(odd, [high], [low], 0, rows), near_mask),
            (side[:rows, :], side[rows : 2 * rows, :], side_mask),
        ]
        total = attend(q_two, blocks)
        if len(refs) > 1:
            total = total + jnp.where(here // 2 == stop - 1, refs[0][...], 0.0)
        o_ref[...] = total


def last_body(pair, parity, own_ref, y_ref, _, came, o_hbm, o_ref, sem):
    rows = o_ref.shape[0]
    couple = lax.axis_index("ctx") // 2
    wanted = couple >= 2
    if parity is not None:
        wanted = wanted & (couple % 2 == parity)

    @pl.when(wanted)
    def _():
        seen = rows_of_first(own_ref[...])
        y = y_ref[pair * rows : (pair + 1) * rows, :] + jnp.where(seen, came[...], 0.0)
        finish(y, o_ref, 0)
        copy = pltpu.make_async_copy(o_ref, o_hbm.at[:, cut(pair)], sem)
        copy.start()
        copy.wait()


def call(body, out, flops, *args, **extra):
    moved = sum(a.size * a.dtype.itemsize for a in args)
    return pl.pallas_call(
        body,
        out_shape=out,
        cost_estimate=pl.CostEstimate(flops=flops, bytes_accessed=moved, transcendentals=0),
        compiler_params=pltpu.CompilerParams(vmem_limit_bytes=GRANT),
        **extra,
    )(*args)


def f32(*shape):
    return jax.ShapeDtypeStruct(shape, jnp.float32)


def per_device(queries, keys, values, doc_ids):
    rows, columns = queries.shape
    assert columns % LANES == 0 and rows == LANES and lax.axis_size("ctx") % 2 == 0
    assert MOST <= 4 * rows
    pairs = columns // LANES
    one = 4 * rows * rows * LANES
    ids = doc_ids.reshape(1, rows)
    held = [pltpu.with_memory_space_constraint(x, pltpu.HBM) for x in (keys, values, queries, ids)]
    load = f32(max(2, pairs) * rows + TILE, LANES)
    y_shape = f32(pairs * rows, LANES)
    every = range(pairs)
    couples = lax.axis_size("ctx") // 2
    stop = couples - 1 if couples > 2 else couples

    def each(moved, arrays):
        out = []
        for pair in every:
            out.append(None if arrays[pair] is None else moved(arrays[pair]))
        return out

    high, low, *rest, own = call(
        functools.partial(pack_body, pairs),
        (load, load, *[f32(2 * rows, LANES)] * (pairs - 1), f32(1, rows)),
        0,
        *held,
        in_specs=[pl.BlockSpec(memory_space=pltpu.HBM)] * 4,
        scratch_shapes=[pltpu.VMEM((rows, columns), x.dtype) for x in (keys, values, queries)]
        + [pltpu.VMEM((1, rows), ids.dtype), pltpu.SemaphoreType.DMA((4,))],
    )
    highs, lows = [high, *rest], [low, *rest]
    got_high = [snake(high, 1, 0)]
    got_low = [snake(low, 0, 0)]
    got = each(lambda x: climb(x, 0, stop), [None, *rest])[1:]
    got_high, got_low = got_high + got, got_low + got
    side = each(trade, lows)
    high_side = each(trade, got_high)
    low_side = [trade(got_low[0]), *high_side[1:]]
    lead = (got_high[0], got_low[0])
    back = []
    for pair in every:
        extra = []
        if pair and stop < couples:
            args = (*lead, own, side[0], rest[pair - 1], side[pair])
            body = functools.partial(top_body, stop, pair)
            extra = [call(body, f32(rows, LANES), 4 * one, *args)]
        args = (*lead, high_side[0], got_high[pair], got_low[pair], high_side[pair], *extra)
        body = functools.partial(far_body, stop, pair)
        far = call(body, f32(rows, LANES), 4 * one, *args)
        if BACK[pair] == "C":
            back.append([(None, climb(far, 1, couples))])
        else:
            evens = exchange(far, 1)
            back.append([(0, evens), (1, exchange(far, 2))])
    out = jax.ShapeDtypeStruct((rows, columns), queries.dtype)
    staged = [pltpu.VMEM(out.shape, out.dtype), pltpu.SemaphoreType.DMA(())]
    here, there = pl.BlockSpec(memory_space=pltpu.VMEM), pl.BlockSpec(memory_space=pltpu.HBM)
    y, partly = call(
        functools.partial(local_body, pairs),
        (y_shape, out),
        4 * pairs * one,
        queries,
        *highs,
        *lows,
        *side,
        out_specs=(here, there),
        scratch_shapes=staged,
    )
    y, partly = call(
        functools.partial(near_body, stop, pairs),
        (y_shape, out),
        4 * pairs * one,
        queries,
        own,
        y,
        partly,
        *got_high,
        *got_low,
        *high_side,
        *low_side,
        in_specs=[here] * 3 + [there] + [here] * (4 * pairs),
        out_specs=(here, there),
        scratch_shapes=staged,
        input_output_aliases={3: 1},
    )
    for pair in every:
        for parity, came in back[pair]:
            partly = call(
                functools.partial(last_body, pair, parity),
                out,
                0,
                own,
                y,
                partly,
                came,
                in_specs=[here, here, there, here],
                out_specs=there,
                scratch_shapes=[pltpu.VMEM((rows, LANES), out.dtype), staged[1]],
                input_output_aliases={2: 0},
            )
    return partly


BACK = 'CT'


def solution(mesh):
    placed = P(("groups", "ctx"), ("heads", "rep"))
    return jax.shard_map(
        per_device,
        mesh=mesh,
        in_specs=(placed, placed, placed, P(("groups", "ctx"))),
        out_specs=placed,
        check_vma=False,
    )
```
